32 devices in a mesh: groups: 1, rec: 32 (over z, y, x, core).
Axes of the slice: x: 2, y: 2, z: 4, core: 2. Of those that a mesh axis runs over, the one named last changes fastest.
Arguments:
- records: bfloat16 [4, 512, 2, 128], P(None, ('groups', 'rec')), may hold values from -6 to 6
- dest: int32 [512, 4], P('groups'), may hold values from 0 to 31, as said below
- w_in: bfloat16 [64, 36], replicated, may hold values from -1 to 1
- b_in: float32 [64], replicated, may hold values from -3 to 3
- w_mid: bfloat16 [64, 64], replicated, may hold values from -0.75 to 0.75
- b_mid: float32 [64], replicated, may hold values from -3 to 3
- w_out: bfloat16 [64, 36], replicated, may hold values from -0.25 to 0.25
Outputs:
- residual: float32 [4, 512, 2, 128], P(None, ('groups', 'rec'))
- grad_w_in: float32 [64, 36], P('groups')
- grad_b_in: float32 [64], P('groups')
- grad_w_mid: float32 [64, 64], P('groups')
- grad_b_mid: float32 [64], P('groups')
- grad_w_out: float32 [64, 36], P('groups')
The draws below stay inside these ranges and needn't reach their ends.
Inputs may be any that keep to these rules, and one draw needn't show every extreme that they name: `dest`: from the 16 blocks of one record device at most 2 copies go to one owner; in every draw one owner receives exactly 2 copies from every record device.
All inputs are finite; a program needn't handle non-finite values.
Results may differ from the reference program's by a relative error of at most 0.0005.
The reference program's roundings to bfloat16 on the way count: a program that leaves them out, or rounds other values in their place, can miss the bound.
Values may be sent and summed in bfloat16 or wider, within the bound.
A program may use at most 192 MiB of HBM per device.

```python
import math
import jax
import jax.numpy as jnp
from jax import lax

C = 64
CMP = 4
VES = 4
CAP = 2
TR = 2
S = 128
CH = 16
BLOCKS = 512
N_REC = 32


def draw_dest(key, part):
    total = VES * CH
    slots = CAP * N_REC
    key_busy, key_rows = jax.random.split(jax.random.fold_in(key, 17))
    busy = jax.random.randint(key_busy, (), 0, N_REC)
    tokens = jnp.arange(slots, dtype=jnp.int32)
    owner = tokens // CAP

    def one_device(row_key):
        key_score, key_perm = jax.random.split(row_key)
        score = jax.random.randint(key_score, (slots,), 0, 1048576) * slots + tokens
        score = jnp.where(owner == busy, tokens - slots, score)
        order = jnp.argsort(score, stable=True)
        chosen = owner[order[:total]]
        return chosen[jax.random.permutation(key_perm, total)]
    rows = jax.vmap(one_device)(jax.random.split(key_rows, N_REC))
    return rows.reshape(N_REC * CH, VES).astype(jnp.int32)


def steps_of(own_key, dims, pieces, low, high):
    gain = 1.0
    for axis_at, shards_of in pieces:
        draws = jax.random.uniform(jax.random.fold_in(jax.random.fold_in(own_key, 6), axis_at), (shards_of,), jnp.float32, low / len(pieces), high / len(pieces))
        gain = gain * jnp.repeat(jnp.exp(draws), dims[axis_at] // shards_of).reshape((-1,) + (1,) * (len(dims) - 1 - axis_at))
    return gain


def normal_values(stream_key, shape, scale, reach, cuts=(), kind=jnp.bfloat16):
    loudness = steps_of(stream_key, shape, cuts, -0.22, 0.18) if cuts else 1.0
    drawn = jax.random.normal(stream_key, shape, jnp.float32) * scale * loudness
    return jnp.minimum(jnp.maximum(drawn, -reach), reach).astype(kind)


def setup_inputs(seed: int = 0, part: int = 0) -> dict:
    arg_keys = jax.random.split(jax.random.key(seed), 8)
    part_keys = jax.random.split(jax.random.fold_in(arg_keys[7], part), 8)
    return {
        "records": normal_values(part_keys[0], (CMP, BLOCKS, TR, S), 1.0, 6.0, ((1, 32),)),
        "dest": draw_dest(jax.random.fold_in(jax.random.fold_in(arg_keys[7], part), 71), part),
        "w_in": normal_values(arg_keys[2], (C, CMP * 9), (CMP * 9) ** -0.5, 1.0),
        "b_in": normal_values(arg_keys[3], (C,), 0.5, 3.0, (), jnp.float32),
        "w_mid": normal_values(arg_keys[4], (C, C), C ** -0.5, 0.75),
        "b_mid": normal_values(arg_keys[5], (C,), 0.5, 3.0, (), jnp.float32),
        "w_out": normal_values(arg_keys[6], (C, CMP * 9), (C * 9) ** -0.5, 0.25),
    }


def patches(field, flip):
    count, height, width = field.shape
    padded = jnp.pad(field, ((0, 0), (1, 1), (1, 1)))
    taps = []
    for row in range(3):
        for col in range(3):
            top = 2 - row if flip else row
            left = 2 - col if flip else col
            taps.append(padded[:, top:top + height, left:left + width])
    return jnp.stack(taps, axis=1).reshape(count * 9, height, width)

def collect(terms, parts):
    height, width = (terms.shape[1], terms.shape[2])
    stacked = jnp.pad(terms.reshape(parts, 9, height, width), ((0, 0), (0, 0), (1, 1), (1, 1)))
    total = jnp.zeros((parts, height, width), jnp.float32)
    for row in range(3):
        for col in range(3):
            total = total + stacked[:, 3 * row + col, row:row + height, col:col + width]
    return total

def silu_grad(z):
    sig = jax.nn.sigmoid(z)
    return sig * (1.0 + z * (1.0 - sig))

def forward(image, w_in, b_in, w_mid, b_mid, w_out):
    inputs = patches(image, False)
    z1 = jnp.einsum('cu,uhw->chw', w_in.astype(jnp.float32), inputs.astype(jnp.float32)) + b_in[:, None, None]
    a1 = jax.nn.silu(z1).astype(jnp.bfloat16)
    z2 = jnp.einsum('dc,chw->dhw', w_mid.astype(jnp.float32), a1.astype(jnp.float32)) + b_mid[:, None, None]
    a2 = jax.nn.silu(z2).astype(jnp.bfloat16)
    terms = jnp.einsum('cu,chw->uhw', w_out.astype(jnp.float32), a2.astype(jnp.float32))
    estimate = collect(terms, image.shape[0])
    return (estimate, (inputs, z1, a1, z2, a2))

def backward(grad_image, w_mid, w_out, saved):
    inputs, z1, a1, z2, a2 = saved
    flipped = patches(grad_image, True).astype(jnp.float32)
    dw_out = jnp.einsum('chw,uhw->cu', a2.astype(jnp.float32), flipped)
    da2 = jnp.einsum('cu,uhw->chw', w_out.astype(jnp.float32), flipped)
    dz2 = (da2 * silu_grad(z2)).astype(jnp.bfloat16).astype(jnp.float32)
    dw_mid = jnp.einsum('dhw,chw->dc', dz2, a1.astype(jnp.float32))
    db_mid = lax.optimization_barrier(jnp.sum(dz2, axis=(1, 2)))
    da1 = jnp.einsum('dc,dhw->chw', w_mid.astype(jnp.float32), dz2)
    dz1 = (da1 * silu_grad(z1)).astype(jnp.bfloat16).astype(jnp.float32)
    dw_in = jnp.einsum('chw,uhw->cu', dz1, inputs.astype(jnp.float32))
    db_in = lax.optimization_barrier(jnp.sum(dz1, axis=(1, 2)))
    return (dw_in, db_in, dw_mid, db_mid, dw_out)

def reference(records, dest, w_in, b_in, w_mid, b_mid, w_out):
    count = N_REC
    items = CH * VES
    table = dest.reshape(count, items).astype(jnp.int32)
    owners = jnp.arange(count, dtype=jnp.int32)
    sources = jnp.arange(count, dtype=jnp.int32)[:, None] * CH + jnp.arange(items, dtype=jnp.int32)[None, :] // VES
    ranks_k = jnp.arange(CAP, dtype=jnp.int32)

    def owner_index(owner):
        hits = (table == owner).astype(jnp.int32)
        ranks = jnp.cumsum(hits, axis=1) - 1
        chosen = hits[:, None, :] * (ranks[:, None, :] == ranks_k[None, :, None]).astype(jnp.int32)
        pick = lax.optimization_barrier(jnp.sum(chosen * sources[:, None, :], axis=2)).reshape(count * CAP)
        valid = lax.optimization_barrier(jnp.sum(chosen, axis=2)).reshape(count * CAP)
        return (pick.astype(jnp.int32), valid)

    def assemble(field, owner):
        pick, valid = owner_index(owner)
        taken = jnp.take(field, pick, axis=1) * valid.astype(field.dtype)[None, :, None, None]
        return taken.reshape(CMP, count * CAP * TR, S)

    def make_estimate(owner):
        estimate, saved = forward(assemble(records, owner), w_in, b_in, w_mid, b_mid, w_out)
        return estimate.astype(jnp.bfloat16).reshape(CMP, count * CAP, TR, S)
    estimates = lax.map(make_estimate, owners)
    hits3 = (table[:, :, None] == owners[None, None, :]).astype(jnp.int32)
    rank = lax.optimization_barrier(jnp.sum((jnp.cumsum(hits3, axis=1) - 1) * hits3, axis=2))
    slot = (jnp.arange(count, dtype=jnp.int32)[:, None] * CAP + rank).reshape(-1).astype(jnp.int32)
    values = estimates[table.reshape(-1), :, slot]
    values = values.astype(jnp.float32).reshape(count, CH, VES, CMP, TR, S)
    reblend = lax.optimization_barrier(jnp.sum(values, axis=2)).reshape(count * CH, CMP, TR, S)
    reblend = jnp.transpose(reblend, (1, 0, 2, 3))
    residual = reblend - records.astype(jnp.float32)
    rounded = residual.astype(jnp.bfloat16)

    def owner_grads(owner):
        estimate, saved = forward(assemble(records, owner), w_in, b_in, w_mid, b_mid, w_out)
        return backward(assemble(rounded, owner), w_mid, w_out, saved)
    terms = lax.map(owner_grads, owners)
    scale = 1.0 / math.sqrt(CMP * BLOCKS * TR * S)
    grads = tuple((lax.optimization_barrier(jnp.sum(term, axis=0)) * scale for term in terms))
    return (residual, grads[0], grads[1], grads[2], grads[3], grads[4])
```

```python
import functools
import math

import jax
import jax.numpy as jnp
from jax import lax
from jax.experimental import pallas as pl
from jax.experimental.pallas import tpu as pltpu
from jax.sharding import PartitionSpec as P

VES = 4
CAP = 2
F32 = jnp.float32
BF16 = jnp.bfloat16
NT = (((1,), (1,)), ((), ()))


def iota(shape, dim):
    return lax.broadcasted_iota(jnp.int32, shape, dim)


def dot(a, b, dims=None):
    if dims is None:
        return jnp.dot(a, b, preferred_element_type=F32)
    return lax.dot_general(a, b, dims, preferred_element_type=F32)


def onehot(mask):
    return jnp.where(mask, 1.0, 0.0).astype(F32)


def tap_of(k, q_out, flip):
    tile, col, trace, comp = k // 64, (k // 16) % 4, (k // 4) % 4, k % 4
    row = 4 * (tile - 1) + trace - q_out + 1
    ok = (row >= 0) & (row <= 2) & (col <= 2) & (tile <= 2)
    if flip:
        row, col = 2 - row, 2 - col
    return jnp.where(ok, 9 * comp + 3 * row + col, -1)


def kernel(
    n, scale, chunk,
    rec_ref, dest_ref, w_in_ref, b_in_ref, w_mid_ref, b_mid_ref, w_out_ref,
    res_ref, grad_ref,
    mine, out1, in1, est, in2, out3, in3, parts, in4, part, in5,
    sel, sel_t, wt1, wt2, wt2_t, wm, wm_t, bias1, bias2,
    xs, qs, acc, a1s, a2s, d1s, d2s, g1, g2, gm, gb,
    dest_sem, send_sem, recv_sem,
):
    me = lax.axis_index("rec")
    blocks = mine.shape[0]

    barrier = pltpu.get_barrier_semaphore()

    def greet(d, _):
        pl.semaphore_signal(
            barrier, inc=1, device_id={"rec": (me + d) % n}, device_id_type=pl.DeviceIdType.MESH
        )
        return 0

    fetch = pltpu.make_async_copy(
        dest_ref.at[pl.ds(pl.multiple_of(me * blocks, blocks), blocks)], mine, dest_sem
    )
    fetch.start()
    lax.fori_loop(1, n, greet, 0)

    def exchange(src, dst, phase):
        def send(d, _):
            peer = (me + d) % n
            pltpu.make_async_remote_copy(
                src_ref=src.at[peer],
                dst_ref=dst.at[me],
                send_sem=send_sem.at[phase],
                recv_sem=recv_sem.at[phase],
                device_id={"rec": peer},
                device_id_type=pl.DeviceIdType.MESH,
            ).start()
            return 0

        lax.fori_loop(1, n, send, 0)
        dst[me] = src[me]

    def arrive(dst, phase):
        whole = dst.at[pl.ds(0, n - 1)]
        pltpu.make_async_copy(whole, whole, recv_sem.at[phase]).wait()

    def sent(src, phase):
        whole = src.at[pl.ds(0, n - 1)]
        pltpu.make_async_copy(whole, whole, send_sem.at[phase]).wait()

    fetch.wait()
    column = iota((blocks, 128), 1)
    item = (column // 2) % blocks
    block = iota((blocks, 128), 0)
    here = [jnp.broadcast_to(mine[:, v : v + 1], (blocks, 128)) for v in range(VES)]
    lane = iota((1, 128), 1)
    inner = (lane % 2) * 4 + lane // 32
    rows = iota((16 * n, 128), 0)
    mask = None
    for v in range(VES):
        own = jnp.sum(jnp.where(block == item, here[v], 0), axis=0, keepdims=True)
        rank = jnp.zeros((blocks, 128), jnp.int32)
        for u in range(VES):
            before = (block <= item) if u < v else (block < item)
            rank = rank + jnp.where(before & (here[u] == own), 1, 0)
        target = (own * CAP + jnp.sum(rank, axis=0, keepdims=True)) * 8 + inner
        hit = rows == target
        mask = hit if mask is None else mask | hit
    picked = onehot(mask)
    sel[...] = picked.astype(BF16)
    out1[...] = dot(sel[...], rec_ref[...]).astype(BF16).reshape(n, 16, 128)
    pl.semaphore_wait(barrier, n - 1)
    exchange(out1, in1, 0)

    sel_t[...] = picked.T.astype(BF16)
    u = iota((36, 256), 0)
    k = iota((36, 256), 1)
    for q in range(4):
        span = slice(64 * q, 64 * q + 64)
        wt1[span] = dot(w_in_ref[...], onehot(u == tap_of(k, q, False)).astype(BF16)).astype(BF16)
        wt2[span] = dot(w_out_ref[...], onehot(u == tap_of(k, q, True)).astype(BF16)).astype(BF16)
    wt2_t[...] = wt2[...].astype(F32).T.astype(BF16)
    tall = onehot(iota((256, 64), 0) % 64 == iota((256, 64), 1)).astype(BF16)
    wide = onehot(iota((64, 256), 1) % 64 == iota((64, 256), 0)).astype(BF16)
    diagonal = iota((256, 256), 0) // 64 == iota((256, 256), 1) // 64
    once = dot(dot(tall, w_mid_ref[...]).astype(BF16), wide)
    once = jnp.where(diagonal, once, 0.0)
    wm[...] = once.astype(BF16)
    wm_t[...] = once.T.astype(BF16)
    near = iota((256, 64), 0) % 64 == iota((256, 64), 1)
    for b_ref, bias in ((b_in_ref, bias1), (b_mid_ref, bias2)):
        values = jnp.sum(jnp.where(near, b_ref[...], 0.0), axis=1, keepdims=True)
        bias[...] = jnp.broadcast_to(values, (256, 128))
    right = iota((128, 256), 1)
    left = iota((128, 256), 0)
    shift = onehot(
        ((right < 128) & (left == right - 1)) | ((right >= 128) & (left == right - 127))
    ).astype(BF16)
    for field in (xs, qs):
        field[:, 0:128] = jnp.zeros((64, 128), BF16)
        field[:, (n + 1) * 128 :] = jnp.zeros((64, 128), BF16)
        field[48:64, :] = onehot(iota((16, (n + 2) * 128), 0) == 0).astype(BF16)
    acc[...] = jnp.zeros_like(acc)
    for g in (g1, g2, gm, gb):
        g[...] = jnp.zeros_like(g)

    def spread(src, field):
        def step(c, _):
            tiles = src[pl.ds(c * 8, 8)].reshape(128, 128)
            moved = dot(tiles, shift).astype(BF16)
            for t in range(8):
                at = pl.ds(pl.multiple_of((c * 8 + t + 1) * 128, 128), 128)
                span = slice(16 * t, 16 * t + 16)
                field[0:16, at] = moved[span, 0:128]
                field[16:32, at] = tiles[span]
                field[32:48, at] = moved[span, 128:256]
            return 0

        lax.fori_loop(0, n // 8, step, 0)

    size = chunk * 128

    def stack(field, c):
        parts_ = [
            field[:, pl.ds(pl.multiple_of(c * size + d * 128, 128), size)] for d in range(3)
        ]
        return jnp.concatenate(parts_ + [jnp.zeros((64, size), BF16)], axis=0)

    def activate(z, a, d, at):
        s = 0.5 * jnp.tanh(0.5 * z) + 0.5
        out = (z * s).astype(BF16)
        a[:, at] = out
        d[:, at] = s * (1.0 + z * (1.0 - s))
        return out

    arrive(in1, 0)
    spread(in1, xs)

    def forward(c, _):
        at = pl.ds(pl.multiple_of(c * size, 128), size)
        b1 = jnp.concatenate([bias1[...]] * chunk, axis=1)
        b2 = jnp.concatenate([bias2[...]] * chunk, axis=1)
        a1 = activate(dot(wt1[...], stack(xs, c)) + b1, a1s, d1s, at)
        a2 = activate(dot(wm[...], a1) + b2, a2s, d2s, at)
        terms = dot(wt2_t[...], a2)
        for d in range(3):
            to = pl.ds(pl.multiple_of(c * size + d * 128, 128), size)
            acc[:, to] = acc[:, to] + terms[64 * d : 64 * d + 48]
        return 0

    lax.fori_loop(0, n // chunk, forward, 0)

    sample = iota((16, 128), 1)

    def close(s, _):
        at = pl.ds(pl.multiple_of((s + 1) * 128, 128), 128)
        before = jnp.where(sample < 127, pltpu.roll(acc[0:16, at], 127, 1), 0.0)
        after = jnp.where(sample > 0, pltpu.roll(acc[32:48, at], 1, 1), 0.0)
        est[s] = (acc[16:32, at] + before + after).astype(BF16)
        return 0

    lax.fori_loop(0, n, close, 0)
    exchange(est, in2, 1)
    arrive(in2, 1)
    residual = dot(sel_t[...], in2[...].reshape(16 * n, 128)) - rec_ref[...].astype(F32)
    res_ref[...] = residual
    out3[...] = dot(sel[...], residual.astype(BF16)).astype(BF16).reshape(n, 16, 128)
    exchange(out3, in3, 2)
    arrive(in3, 2)
    spread(in3, qs)

    def backward(c, _):
        at = pl.ds(pl.multiple_of(c * size, 128), size)
        field = stack(qs, c)
        g2[...] += dot(a2s[:, at], field, NT)
        dz2 = dot(wt2[...], field) * d2s[:, at]
        dz2 = dz2.astype(BF16)
        for t in range(chunk):
            gb[...] += dz2[:, 128 * t : 128 * t + 128].astype(F32)
        gm[...] += dot(dz2, a1s[:, at], NT)
        dz1 = (dot(wm_t[...], dz2) * d1s[:, at]).astype(BF16)
        g1[...] += dot(dz1, stack(xs, c), NT)
        return 0

    lax.fori_loop(0, n // chunk, backward, 0)

    lane = iota((64, 128), 1)
    deep = iota((256, 128), 0)
    across = iota((256, 128), 1)
    first = jnp.zeros((64, 128), F32)
    for q in range(4):
        span = slice(64 * q, 64 * q + 64)
        for g, fold in (
            (g1, (across == tap_of(deep, q, False)) | ((deep == 112) & (across == 36))),
            (g2, across - 64 == jnp.where(tap_of(deep, q, True) < 0, -100, tap_of(deep, q, True))),
        ):
            x = g[span]
            high = x.astype(BF16)
            rest = x - high.astype(F32)
            middle = rest.astype(BF16)
            low = (rest - middle.astype(F32)).astype(BF16)
            three = dot(jnp.concatenate([high, middle, low], axis=0), onehot(fold).astype(BF16))
            first = first + (three[0:64] + three[64:128] + three[128:192])
    square = jnp.where(diagonal, gm[...], 0.0)
    square = square[0:64] + square[64:128] + square[128:192] + square[192:256]
    square = square[:, 0:128] + square[:, 128:256]
    square = square + pltpu.roll(square, 64, 1)
    summed = jnp.sum(gb[...], axis=1, keepdims=True)
    summed = summed[0:64] + summed[64:128] + summed[128:192] + summed[192:256]
    second = jnp.where(lane < 64, square, jnp.where(lane == 64, summed, 0.0))
    per = 128 // n
    for i in range(n):
        source = first if i * per < 64 else second
        start = (i * per) % 64
        parts[i] = source[start : start + per]

    exchange(parts, in4, 3)
    arrive(in4, 3)
    part[...] = jnp.sum(in4[...], axis=0, keepdims=True) * scale

    def share(d, _):
        peer = (me + d) % n
        pltpu.make_async_remote_copy(
            src_ref=part.at[0],
            dst_ref=in5.at[me],
            send_sem=send_sem.at[4],
            recv_sem=recv_sem.at[4],
            device_id={"rec": peer},
            device_id_type=pl.DeviceIdType.MESH,
        ).start()
        return 0

    lax.fori_loop(1, n, share, 0)
    in5[me] = part[0]
    arrive(in5, 4)
    for i in range(n):
        grad_ref[per * i : per * i + per] = in5[i]
    sent(out1, 0)
    sent(est, 1)
    sent(out3, 2)
    sent(parts, 3)
    sent(in5, 4)


def local(n, records, dest, w_in, b_in, w_mid, b_mid, w_out):
    parts, blocks, traces, samples = records.shape
    width = n * samples
    per = 128 // n
    chunk = 4
    scale = 1.0 / math.sqrt(parts * blocks * n * traces * samples)
    vmem = pl.BlockSpec(memory_space=pltpu.VMEM)
    V = pltpu.VMEM
    message = V((n, 16, 128), BF16)
    piece = V((n, per, 128), F32)
    residual, grads = pl.pallas_call(
        functools.partial(kernel, n, scale, chunk),
        out_shape=(
            jax.ShapeDtypeStruct((128, 128), F32),
            jax.ShapeDtypeStruct((128, 128), F32),
        ),
        in_specs=[vmem, pl.BlockSpec(memory_space=pl.ANY)] + [vmem] * 5,
        out_specs=(vmem, vmem),
        scratch_shapes=[
            V((blocks, VES), jnp.int32),
            message, message, message, message, message, message,
            piece, piece, V((1, per, 128), F32), piece,
            V((16 * n, 128), BF16), V((128, 16 * n), BF16),
            V((256, 256), BF16), V((256, 256), BF16), V((256, 256), BF16),
            V((256, 256), BF16), V((256, 256), BF16),
            V((256, 128), F32), V((256, 128), F32),
            V((64, width + 256), BF16), V((64, width + 256), BF16), V((48, width + 256), F32),
            V((256, width), BF16), V((256, width), BF16), V((256, width), F32), V((256, width), F32),
            V((256, 256), F32), V((256, 256), F32), V((256, 256), F32), V((256, 128), F32),
            pltpu.SemaphoreType.DMA, pltpu.SemaphoreType.DMA((5,)), pltpu.SemaphoreType.DMA((5,)),
        ],
        compiler_params=pltpu.CompilerParams(
            collective_id=0, has_side_effects=True, vmem_limit_bytes=63 * 1024 * 1024
        ),
        name="deblend",
    )(
        records.reshape(128, 128), dest, w_in, b_in.reshape(1, 64), w_mid, b_mid.reshape(1, 64), w_out
    )
    return (
        residual.reshape(records.shape),
        grads[0:64, 0:36],
        grads[0:64, 36],
        grads[64:128, 0:64],
        grads[64:128, 64],
        grads[0:64, 64:100],
    )


def solution(mesh):
    return jax.shard_map(
        functools.partial(local, mesh.shape["rec"]),
        mesh=mesh,
        in_specs=(
            P(None, ("groups", "rec"), None, None),
            P("groups", None),
            P(),
            P(),
            P(),
            P(),
            P(),
        ),
        out_specs=(
            P(None, ("groups", "rec"), None, None),
            P("groups", None),
            P("groups"),
            P("groups", None),
            P("groups"),
            P("groups", None),
        ),
        check_vma=False,
    )
```

```python
import functools
import math

import jax
import jax.numpy as jnp
from jax import lax
from jax.experimental import pallas as pl
from jax.experimental.pallas import tpu as pltpu
from jax.sharding import PartitionSpec as P

VES = 4
CAP = 2
F32 = jnp.float32
BF16 = jnp.bfloat16
NT = (((1,), (1,)), ((), ()))
TN = (((0,), (0,)), ((), ()))


def iota(shape, dim):
    return lax.broadcasted_iota(jnp.int32, shape, dim)


def dot(a, b, dims=None):
    if dims is None:
        return jnp.dot(a, b, preferred_element_type=F32)
    return lax.dot_general(a, b, dims, preferred_element_type=F32)


def onehot(mask):
    return jnp.where(mask, 1.0, 0.0).astype(F32)


def tap_of(k, q_out, flip):
    tile, col, trace, comp = k >> 6, (k >> 4) & 3, (k >> 2) & 3, k & 3
    row = 4 * (tile - 1) + trace - q_out + 1
    ok = (row >= 0) & (row <= 2) & (col <= 2) & (tile <= 2)
    if flip:
        row, col = 2 - row, 2 - col
    return jnp.where(ok, 9 * comp + 3 * row + col, -1)


def kernel(
    n, scale, chunk,
    rec_ref, dest_ref, w_in_ref, b_in_ref, w_mid_ref, b_mid_ref, w_out_ref,
    res_ref, grad_ref,
    out1, in1, est, in2, out3, in3, parts, in4, part, in5,
    sel, sel_t, wt1, wt2, wt2_t, wm, wm_t, bias1, bias2,
    xs, qs, acc, a1s, a2s, d1s, d2s, g1, g2, gm, gb, fold1, fold2,
    send_sem, recv_sem,
):
    me = lax.axis_index("rec")
    blocks = rec_ref.shape[0] // 8

    barrier = pltpu.get_barrier_semaphore()

    def greet(d, _):
        pl.semaphore_signal(
            barrier, inc=1, device_id={"rec": (me + d) % n}, device_id_type=pl.DeviceIdType.MESH
        )
        return 0

    lax.fori_loop(1, n, greet, 0, unroll=True)

    def exchange(src, dst, phase):
        def send(d, _):
            peer = (me + d) % n
            pltpu.make_async_remote_copy(
                src_ref=src.at[peer],
                dst_ref=dst.at[me],
                send_sem=send_sem.at[phase],
                recv_sem=recv_sem.at[phase],
                device_id={"rec": peer},
                device_id_type=pl.DeviceIdType.MESH,
            ).start()
            return 0

        lax.fori_loop(1, n, send, 0, unroll=True)
        dst[me] = src[me]

    def arrive(dst, phase):
        every = dst.at[pl.ds(0, n - 1)]
        pltpu.make_async_copy(every, every, recv_sem.at[phase]).wait()

    def sent(src, phase):
        every = src.at[pl.ds(0, n - 1)]
        pltpu.make_async_copy(every, every, send_sem.at[phase]).wait()

    column = iota((blocks, 128), 1)
    item = (column >> 1) % blocks
    block = iota((blocks, 128), 0)
    length = dest_ref.shape[1]
    wanted = iota((blocks, length), 1) - iota((blocks, length), 0) == me * blocks
    here = [
        jnp.broadcast_to(
            jnp.sum(jnp.where(wanted, dest_ref[v : v + 1], 0), axis=1, keepdims=True), (blocks, 128)
        )
        for v in range(VES)
    ]
    lane = iota((1, 128), 1)
    inner = (lane & 1) * 4 + (lane >> 5)
    rows = iota((16 * n, 128), 0)
    mask = None
    for v in range(VES):
        own = jnp.sum(jnp.where(block == item, here[v], 0), axis=0, keepdims=True)
        rank = jnp.zeros((blocks, 128), jnp.int32)
        for u in range(VES):
            before = (block <= item) if u < v else (block < item)
            rank = rank + jnp.where(before & (here[u] == own), 1, 0)
        target = (own * CAP + jnp.sum(rank, axis=0, keepdims=True)) * 8 + inner
        hit = rows == target
        mask = hit if mask is None else mask | hit
    picked = onehot(mask)
    sel[...] = picked.astype(BF16)
    out1[...] = dot(sel[...], rec_ref[...]).astype(BF16).reshape(n, 16, 128)
    pl.semaphore_wait(barrier, n - 1)
    exchange(out1, in1, 0)

    sel_t[...] = picked.T.astype(BF16)
    u = iota((36, 256), 0)
    k = iota((36, 256), 1)
    for q in range(4):
        span = slice(64 * q, 64 * q + 64)
        wt1[span] = dot(w_in_ref[...], onehot(u == tap_of(k, q, False)).astype(BF16), TN).astype(BF16)
        wt2[span] = dot(w_out_ref[...], onehot(u == tap_of(k, q, True)).astype(BF16), TN).astype(BF16)
    wt2_t[...] = wt2[...].astype(F32).T.astype(BF16)
    tall = onehot((iota((256, 64), 0) & 63) == iota((256, 64), 1)).astype(BF16)
    wide = onehot((iota((64, 256), 1) & 63) == iota((64, 256), 0)).astype(BF16)
    diagonal = iota((256, 256), 0) >> 6 == iota((256, 256), 1) >> 6
    once = dot(dot(tall, w_mid_ref[...]).astype(BF16), wide)
    once = jnp.where(diagonal, once, 0.0)
    wm[...] = once.astype(BF16)
    wm_t[...] = once.T.astype(BF16)
    near = (iota((256, 64), 0) & 63) == iota((256, 64), 1)
    for b_ref, bias in ((b_in_ref, bias1), (b_mid_ref, bias2)):
        values = jnp.sum(jnp.where(near, b_ref[...], 0.0), axis=1, keepdims=True)
        bias[...] = jnp.broadcast_to(values, (256, 128))
    right = iota((128, 256), 1)
    left = iota((128, 256), 0)
    shift = onehot(
        ((right < 128) & (left == right - 1)) | ((right >= 128) & (left == right - 127))
    ).astype(BF16)
    for field in (xs, qs):
        field[:, 0:128] = jnp.zeros((64, 128), BF16)
        field[:, (n + 1) * 128 :] = jnp.zeros((64, 128), BF16)
        field[48:64, :] = onehot(iota((16, (n + 2) * 128), 0) == 0).astype(BF16)
    acc[...] = jnp.zeros_like(acc)
    for g in (g1, g2, gm, gb):
        g[...] = jnp.zeros_like(g)

    def spread(src, field):
        def step(c, _):
            tiles = src[pl.ds(c * 8, 8)].reshape(128, 128)
            moved = dot(tiles, shift).astype(BF16)
            for t in range(8):
                at = pl.ds(pl.multiple_of((c * 8 + t + 1) * 128, 128), 128)
                span = slice(16 * t, 16 * t + 16)
                field[0:16, at] = moved[span, 0:128]
                field[16:32, at] = tiles[span]
                field[32:48, at] = moved[span, 128:256]
            return 0

        lax.fori_loop(0, n // 8, step, 0, unroll=4)

    size = chunk * 128

    def stack(field, c):
        parts_ = [
            field[:, pl.ds(pl.multiple_of(c * size + d * 128, 128), size)] for d in range(3)
        ]
        return jnp.concatenate(parts_ + [jnp.zeros((64, size), BF16)], axis=0)

    def activate(z, a, d, at):
        s = 0.5 * jnp.tanh(0.5 * z) + 0.5
        out = (z * s).astype(BF16)
        a[:, at] = out
        d[:, at] = s * (1.0 + z * (1.0 - s))
        return out

    arrive(in1, 0)
    spread(in1, xs)

    def forward(c, _):
        at = pl.ds(pl.multiple_of(c * size, 128), size)
        b1 = jnp.concatenate([bias1[...]] * chunk, axis=1)
        b2 = jnp.concatenate([bias2[...]] * chunk, axis=1)
        a1 = activate(dot(wt1[...], stack(xs, c)) + b1, a1s, d1s, at)
        a2 = activate(dot(wm[...], a1) + b2, a2s, d2s, at)
        terms = dot(wt2_t[...], a2)
        for d in range(3):
            to = pl.ds(pl.multiple_of(c * size + d * 128, 128), size)
            acc[:, to] = acc[:, to] + terms[64 * d : 64 * d + 48]
        return 0

    lax.fori_loop(0, n // chunk, forward, 0)

    sample = iota((16, 128), 1)

    def close(s, _):
        at = pl.ds(pl.multiple_of((s + 1) * 128, 128), 128)
        before = jnp.where(sample < 127, pltpu.roll(acc[0:16, at], 127, 1), 0.0)
        after = jnp.where(sample > 0, pltpu.roll(acc[32:48, at], 1, 1), 0.0)
        est[s] = (acc[16:32, at] + before + after).astype(BF16)
        return 0

    lax.fori_loop(0, n, close, 0, unroll=8)
    exchange(est, in2, 1)
    deep = iota((256, 128), 0)
    across = iota((256, 128), 1)
    for q in range(4):
        tap = tap_of(deep, q, True)
        fold1[q] = onehot(
            (across == tap_of(deep, q, False)) | ((deep == 112) & (across == 36))
        ).astype(BF16)
        fold2[q] = onehot((across - 64 == tap) & (tap >= 0)).astype(BF16)
    arrive(in2, 1)
    residual = dot(sel_t[...], in2[...].reshape(16 * n, 128)) - rec_ref[...].astype(F32)
    res_ref[...] = residual
    out3[...] = dot(sel[...], residual.astype(BF16)).astype(BF16).reshape(n, 16, 128)
    exchange(out3, in3, 2)
    arrive(in3, 2)
    spread(in3, qs)

    def backward(c, _):
        at = pl.ds(pl.multiple_of(c * size, 128), size)
        field = stack(qs, c)
        g2[...] += dot(a2s[:, at], field, NT)
        dz2 = dot(wt2[...], field) * d2s[:, at]
        dz2 = dz2.astype(BF16)
        for t in range(chunk):
            gb[...] += dz2[:, 128 * t : 128 * t + 128].astype(F32)
        gm[...] += dot(dz2, a1s[:, at], NT)
        dz1 = (dot(wm_t[...], dz2) * d1s[:, at]).astype(BF16)
        g1[...] += dot(dz1, stack(xs, c), NT)
        return 0

    lax.fori_loop(0, n // chunk, backward, 0)

    lane = iota((64, 128), 1)
    first = jnp.zeros((64, 128), F32)
    for q in range(4):
        span = slice(64 * q, 64 * q + 64)
        for g, fold in ((g1, fold1), (g2, fold2)):
            x = g[span]
            high = x.astype(BF16)
            rest = x - high.astype(F32)
            middle = rest.astype(BF16)
            low = (rest - middle.astype(F32)).astype(BF16)
            three = dot(jnp.concatenate([high, middle, low], axis=0), fold[q])
            first = first + (three[0:64] + three[64:128] + three[128:192])
    square = jnp.where(diagonal, gm[...], 0.0)
    square = square[0:64] + square[64:128] + square[128:192] + square[192:256]
    square = square[:, 0:128] + square[:, 128:256]
    square = square + pltpu.roll(square, 64, 1)
    summed = jnp.sum(gb[...], axis=1, keepdims=True)
    summed = summed[0:64] + summed[64:128] + summed[128:192] + summed[192:256]
    first = jnp.where(lane == 37, summed, first)
    first = jnp.concatenate([first, jnp.zeros((64, 128), F32)], axis=0).T
    total = [first[0:64] + jnp.where(lane >= 64, square, 0.0), first[64:128]]
    per = 128 // n
    for i in range(n):
        start = (i * per) % 64
        parts[i] = total[i * per // 64][start : start + per]

    exchange(parts, in4, 3)
    arrive(in4, 3)
    part[...] = jnp.sum(in4[...], axis=0, keepdims=True) * scale

    def share(d, _):
        peer = (me + d) % n
        pltpu.make_async_remote_copy(
            src_ref=part.at[0],
            dst_ref=in5.at[me],
            send_sem=send_sem.at[4],
            recv_sem=recv_sem.at[4],
            device_id={"rec": peer},
            device_id_type=pl.DeviceIdType.MESH,
        ).start()
        return 0

    lax.fori_loop(1, n, share, 0, unroll=True)
    in5[me] = part[0]
    arrive(in5, 4)
    for i in range(n):
        grad_ref[per * i : per * i + per] = in5[i]
    sent(out1, 0)
    sent(est, 1)
    sent(out3, 2)
    sent(parts, 3)
    sent(in5, 4)


def deal(res_ref, grad_ref, out_ref, dwi_ref, dbi_ref, dwm_ref, dbm_ref, dwo_ref):
    out_ref[...] = res_ref[...]
    dwi_ref[...] = grad_ref[0:36, 0:64]
    dbi_ref[...] = grad_ref[36:37, 0:64]
    dbm_ref[...] = grad_ref[37:38, 0:64]
    dwo_ref[...] = grad_ref[64:100, 0:64]
    dwm_ref[...] = pltpu.roll(grad_ref[0:64], 64, 1)[:, 0:64]


def local(n, records, dest, w_in, b_in, w_mid, b_mid, w_out):
    parts, blocks, traces, samples = records.shape
    width = n * samples
    per = 128 // n
    chunk = 4
    scale = 1.0 / math.sqrt(parts * blocks * n * traces * samples)
    vmem = pl.BlockSpec(memory_space=pltpu.VMEM)
    V = pltpu.VMEM
    message = V((n, 16, 128), BF16)
    piece = V((n, per, 128), F32)
    result = pl.pallas_call(
        functools.partial(kernel, n, scale, chunk),
        out_shape=(
            jax.ShapeDtypeStruct((128, 128), F32),
            jax.ShapeDtypeStruct((128, 128), F32),
        ),
        in_specs=[vmem] * 7,
        out_specs=(vmem,) * 2,
        scratch_shapes=[
            message, message, message, message, message, message,
            piece, piece, V((1, per, 128), F32), piece,
            V((16 * n, 128), BF16), V((128, 16 * n), BF16),
            V((256, 256), BF16), V((256, 256), BF16), V((256, 256), BF16),
            V((256, 256), BF16), V((256, 256), BF16),
            V((256, 128), F32), V((256, 128), F32),
            V((64, width + 256), BF16), V((64, width + 256), BF16), V((48, width + 256), F32),
            V((256, width), BF16), V((256, width), BF16), V((256, width), F32), V((256, width), F32),
            V((256, 256), F32), V((256, 256), F32), V((256, 256), F32), V((256, 128), F32),
            V((4, 256, 128), BF16), V((4, 256, 128), BF16),
            pltpu.SemaphoreType.DMA((5,)), pltpu.SemaphoreType.DMA((5,)),
        ],
        compiler_params=pltpu.CompilerParams(
            collective_id=0, has_side_effects=True, vmem_limit_bytes=63 << 20
        ),
        name="deblend",
    )(
        records.reshape(128, 128), dest.T, w_in.T, b_in.reshape(1, 64), w_mid, b_mid.reshape(1, 64), w_out.T
    )
    residual, dwi, dbi, dwm, dbm, dwo = pl.pallas_call(
        deal,
        out_shape=(
            jax.ShapeDtypeStruct((128, 128), F32),
            jax.ShapeDtypeStruct((36, 64), F32),
            jax.ShapeDtypeStruct((1, 64), F32),
            jax.ShapeDtypeStruct((64, 64), F32),
            jax.ShapeDtypeStruct((1, 64), F32),
            jax.ShapeDtypeStruct((36, 64), F32),
        ),
        in_specs=[vmem] * 2,
        out_specs=(vmem,) * 6,
        name="deal",
    )(*result)
    return (
        residual.reshape(records.shape),
        dwi.T,
        dbi.reshape(64),
        dwm,
        dbm.reshape(64),
        dwo.T,
    )


def solution(mesh):
    return jax.shard_map(
        functools.partial(local, mesh.shape["rec"]),
        mesh=mesh,
        in_specs=(
            P(None, ("groups", "rec"), None, None),
            P("groups", None),
            P(),
            P(),
            P(),
            P(),
            P(),
        ),
        out_specs=(
            P(None, ("groups", "rec"), None, None),
            P("groups", None),
            P("groups"),
            P("groups", None),
            P("groups"),
            P("groups", None),
        ),
        check_vma=False,
    )
```

```python
import functools
import math

import jax
import jax.numpy as jnp
from jax import lax
from jax.experimental import pallas as pl
from jax.experimental.pallas import tpu as pltpu
from jax.sharding import PartitionSpec as P

VES = 4
CAP = 2
F32 = jnp.float32
BF16 = jnp.bfloat16
NT = (((1,), (1,)), ((), ()))
TN = (((0,), (0,)), ((), ()))


def iota(shape, dim):
    return lax.broadcasted_iota(jnp.int32, shape, dim)


def dot(a, b, dims=None):
    if dims is None:
        return jnp.dot(a, b, preferred_element_type=F32)
    return lax.dot_general(a, b, dims, preferred_element_type=F32)


def onehot(mask):
    return jnp.where(mask, 1.0, 0.0).astype(F32)


def tap_of(k, q_out, flip):
    tile, col, trace, comp = k >> 6, (k >> 4) & 3, (k >> 2) & 3, k & 3
    row = 4 * (tile - 1) + trace - q_out + 1
    ok = (row >= 0) & (row <= 2) & (col <= 2) & (tile <= 2)
    if flip:
        row, col = 2 - row, 2 - col
    return jnp.where(ok, 9 * comp + 3 * row + col, -1)


def kernel(
    n, scale, chunk,
    rec_ref, dest_ref, w_in_ref, b_in_ref, w_mid_ref, b_mid_ref, w_out_ref,
    res_ref, grad_ref,
    out1, in1, est, in2, out3, in3, parts, in4, part, in5,
    sel, sel_t, wt1, wt2, wt2_t, wm, wm_t, bias1, bias2,
    xs, qs, acc, a1s, a2s, d1s, d2s, g1, g2, gm, gb, fold1, fold2,
    send_sem, recv_sem,
):
    me = lax.axis_index("rec")
    blocks = rec_ref.shape[0] // 8

    barrier = pltpu.get_barrier_semaphore()

    def greet(d, _):
        pl.semaphore_signal(
            barrier, inc=1, device_id={"rec": (me + d) % n}, device_id_type=pl.DeviceIdType.MESH
        )
        return 0

    lax.fori_loop(1, n, greet, 0, unroll=True)

    def exchange(src, dst, phase):
        def send(d, _):
            peer = (me + d) % n
            pltpu.make_async_remote_copy(
                src_ref=src.at[peer],
                dst_ref=dst.at[me],
                send_sem=send_sem.at[phase],
                recv_sem=recv_sem.at[phase],
                device_id={"rec": peer},
                device_id_type=pl.DeviceIdType.MESH,
            ).start()
            return 0

        lax.fori_loop(1, n, send, 0, unroll=True)
        dst[me] = src[me]

    def arrive(dst, phase):
        every = dst.at[pl.ds(0, n - 1)]
        pltpu.make_async_copy(every, every, recv_sem.at[phase]).wait()

    def sent(src, phase):
        every = src.at[pl.ds(0, n - 1)]
        pltpu.make_async_copy(every, every, send_sem.at[phase]).wait()

    column = iota((blocks, 128), 1)
    item = (column >> 1) % blocks
    block = iota((blocks, 128), 0)
    length = dest_ref.shape[1]
    wanted = iota((blocks, length), 1) - iota((blocks, length), 0) == me * blocks
    here = [
        jnp.broadcast_to(
            jnp.sum(jnp.where(wanted, dest_ref[v : v + 1], 0), axis=1, keepdims=True), (blocks, 128)
        )
        for v in range(VES)
    ]
    lane = iota((1, 128), 1)
    inner = (lane & 1) * 4 + (lane >> 5)
    rows = iota((16 * n, 128), 0)
    mask = None
    for v in range(VES):
        own = jnp.sum(jnp.where(block == item, here[v], 0), axis=0, keepdims=True)
        rank = jnp.zeros((blocks, 128), jnp.int32)
        for u in range(VES):
            before = (block <= item) if u < v else (block < item)
            rank = rank + jnp.where(before & (here[u] == own), 1, 0)
        target = (own * CAP + jnp.sum(rank, axis=0, keepdims=True)) * 8 + inner
        hit = rows == target
        mask = hit if mask is None else mask | hit
    picked = onehot(mask)
    sel[...] = picked.astype(BF16)
    out1[...] = dot(sel[...], rec_ref[...]).astype(BF16).reshape(n, 16, 128)
    pl.semaphore_wait(barrier, n - 1)
    exchange(out1, in1, 0)

    sel_t[...] = picked.T.astype(BF16)
    u = iota((36, 256), 0)
    k = iota((36, 256), 1)
    for q in range(4):
        span = slice(64 * q, 64 * q + 64)
        wt1[span] = dot(w_in_ref[...], onehot(u == tap_of(k, q, False)).astype(BF16), TN).astype(BF16)
        wt2[span] = dot(w_out_ref[...], onehot(u == tap_of(k, q, True)).astype(BF16), TN).astype(BF16)
    wt2_t[...] = wt2[...].astype(F32).T.astype(BF16)
    tall = onehot((iota((256, 64), 0) & 63) == iota((256, 64), 1)).astype(BF16)
    wide = onehot((iota((64, 256), 1) & 63) == iota((64, 256), 0)).astype(BF16)
    diagonal = iota((256, 256), 0) >> 6 == iota((256, 256), 1) >> 6
    once = dot(dot(tall, w_mid_ref[...]).astype(BF16), wide)
    once = jnp.where(diagonal, once, 0.0)
    wm[...] = once.astype(BF16)
    wm_t[...] = once.T.astype(BF16)
    near = (iota((256, 64), 0) & 63) == iota((256, 64), 1)
    for b_ref, bias in ((b_in_ref, bias1), (b_mid_ref, bias2)):
        values = jnp.sum(jnp.where(near, b_ref[...], 0.0), axis=1, keepdims=True)
        bias[...] = jnp.broadcast_to(values, (256, 128))
    right = iota((128, 256), 1)
    left = iota((128, 256), 0)
    shift = onehot(
        ((right < 128) & (left == right - 1)) | ((right >= 128) & (left == right - 127))
    ).astype(BF16)
    for field in (xs, qs):
        field[:, 0:128] = jnp.zeros((64, 128), BF16)
        field[:, (n + 1) * 128 :] = jnp.zeros((64, 128), BF16)
        field[48:64, :] = onehot(iota((16, (n + 2) * 128), 0) == 0).astype(BF16)
    acc[...] = jnp.zeros_like(acc)
    for g in (g1, g2, gm, gb):
        g[...] = jnp.zeros_like(g)

    def spread(src, field):
        def step(c, _):
            tiles = src[pl.ds(c * 8, 8)].reshape(128, 128)
            moved = dot(tiles, shift).astype(BF16)
            for t in range(8):
                at = pl.ds(pl.multiple_of((c * 8 + t + 1) * 128, 128), 128)
                span = slice(16 * t, 16 * t + 16)
                field[0:16, at] = moved[span, 0:128]
                field[16:32, at] = tiles[span]
                field[32:48, at] = moved[span, 128:256]
            return 0

        lax.fori_loop(0, n // 8, step, 0, unroll=4)

    size = chunk * 128

    def stack(field, c):
        parts_ = [
            field[:, pl.ds(pl.multiple_of(c * size + d * 128, 128), size)] for d in range(3)
        ]
        return jnp.concatenate(parts_ + [jnp.zeros((64, size), BF16)], axis=0)

    def activate(z, a, d, at):
        s = 0.5 * jnp.tanh(0.5 * z) + 0.5
        out = (z * s).astype(BF16)
        a[:, at] = out
        d[:, at] = s * (1.0 + z * (1.0 - s))
        return out

    arrive(in1, 0)
    spread(in1, xs)

    def forward(c, _):
        at = pl.ds(pl.multiple_of(c * size, 128), size)
        b1 = jnp.concatenate([bias1[...]] * chunk, axis=1)
        b2 = jnp.concatenate([bias2[...]] * chunk, axis=1)
        a1 = activate(dot(wt1[...], stack(xs, c)) + b1, a1s, d1s, at)
        a2 = activate(dot(wm[...], a1) + b2, a2s, d2s, at)
        terms = dot(wt2_t[...], a2)
        for d in range(3):
            to = pl.ds(pl.multiple_of(c * size + d * 128, 128), size)
            acc[:, to] = acc[:, to] + terms[64 * d : 64 * d + 48]
        return 0

    lax.fori_loop(0, n // chunk, forward, 0)

    sample = iota((16, 128), 1)

    def close(s, _):
        at = pl.ds(pl.multiple_of((s + 1) * 128, 128), 128)
        before = jnp.where(sample < 127, pltpu.roll(acc[0:16, at], 127, 1), 0.0)
        after = jnp.where(sample > 0, pltpu.roll(acc[32:48, at], 1, 1), 0.0)
        est[s] = (acc[16:32, at] + before + after).astype(BF16)
        return 0

    lax.fori_loop(0, n, close, 0, unroll=8)
    exchange(est, in2, 1)
    deep = iota((256, 128), 0)
    across = iota((256, 128), 1)
    for q in range(4):
        tap = tap_of(deep, q, True)
        fold1[q] = onehot(
            (across == tap_of(deep, q, False)) | ((deep == 112) & (across == 36))
        ).astype(BF16)
        fold2[q] = onehot((across - 64 == tap) & (tap >= 0)).astype(BF16)
    arrive(in2, 1)
    residual = dot(sel_t[...], in2[...].reshape(16 * n, 128)) - rec_ref[...].astype(F32)
    res_ref[...] = residual
    out3[...] = dot(sel[...], residual.astype(BF16)).astype(BF16).reshape(n, 16, 128)
    exchange(out3, in3, 2)
    arrive(in3, 2)
    spread(in3, qs)

    def backward(c, _):
        at = pl.ds(pl.multiple_of(c * size, 128), size)
        field = stack(qs, c)
        g2[...] += dot(a2s[:, at], field, NT)
        dz2 = dot(wt2[...], field) * d2s[:, at]
        dz2 = dz2.astype(BF16)
        for t in range(chunk):
            gb[...] += dz2[:, 128 * t : 128 * t + 128].astype(F32)
        gm[...] += dot(dz2, a1s[:, at], NT)
        dz1 = (dot(wm_t[...], dz2) * d1s[:, at]).astype(BF16)
        g1[...] += dot(dz1, stack(xs, c), NT)
        return 0

    lax.fori_loop(0, n // chunk, backward, 0)

    lane = iota((64, 128), 1)
    first = jnp.zeros((64, 128), F32)
    for q in range(4):
        span = slice(64 * q, 64 * q + 64)
        for g, fold in ((g1, fold1), (g2, fold2)):
            x = g[span]
            high = x.astype(BF16)
            rest = x - high.astype(F32)
            middle = rest.astype(BF16)
            low = (rest - middle.astype(F32)).astype(BF16)
            three = dot(jnp.concatenate([high, middle, low], axis=0), fold[q])
            first = first + (three[0:64] + three[64:128] + three[128:192])
    square = jnp.where(diagonal, gm[...], 0.0)
    square = square[0:64] + square[64:128] + square[128:192] + square[192:256]
    square = square[:, 0:128] + square[:, 128:256]
    square = square + pltpu.roll(square, 64, 1)
    summed = jnp.sum(gb[...], axis=1, keepdims=True)
    summed = summed[0:64] + summed[64:128] + summed[128:192] + summed[192:256]
    first = jnp.where(lane == 37, summed, first)
    first = jnp.concatenate([first, jnp.zeros((64, 128), F32)], axis=0).T
    total = [first[0:64] + jnp.where(lane >= 64, square, 0.0), first[64:128]]
    per = 128 // n
    for i in range(n):
        start = (i * per) % 64
        parts[i] = total[i * per // 64][start : start + per]

    exchange(parts, in4, 3)
    arrive(in4, 3)
    part[...] = jnp.sum(in4[...], axis=0, keepdims=True) * scale

    def share(d, _):
        peer = (me + d) % n
        pltpu.make_async_remote_copy(
            src_ref=part.at[0],
            dst_ref=in5.at[me],
            send_sem=send_sem.at[4],
            recv_sem=recv_sem.at[4],
            device_id={"rec": peer},
            device_id_type=pl.DeviceIdType.MESH,
        ).start()
        return 0

    lax.fori_loop(1, n, share, 0, unroll=True)
    in5[me] = part[0]
    arrive(in5, 4)
    for i in range(n):
        grad_ref[per * i : per * i + per] = in5[i]
    sent(out1, 0)
    sent(est, 1)
    sent(out3, 2)
    sent(parts, 3)
    sent(in5, 4)


def deal(res_ref, grad_ref, out_ref, dwi_ref, dbi_ref, dwm_ref, dbm_ref, dwo_ref):
    out_ref[...] = res_ref[...]
    dwi_ref[...] = grad_ref[0:36, 0:64]
    dbi_ref[...] = grad_ref[36:37, 0:64]
    dbm_ref[...] = grad_ref[37:38, 0:64]
    dwo_ref[...] = grad_ref[64:100, 0:64]
    dwm_ref[...] = pltpu.roll(grad_ref[0:64], 64, 1)[:, 0:64]


def local(n, records, dest, w_in, b_in, w_mid, b_mid, w_out):
    parts, blocks, traces, samples = records.shape
    width = n * samples
    per = 128 // n
    chunk = max(4, 512 // n)
    scale = 1.0 / math.sqrt(parts * blocks * n * traces * samples)
    vmem = pl.BlockSpec(memory_space=pltpu.VMEM)
    V = pltpu.VMEM
    message = V((n, 16, 128), BF16)
    piece = V((n, per, 128), F32)
    result = pl.pallas_call(
        functools.partial(kernel, n, scale, chunk),
        out_shape=(
            jax.ShapeDtypeStruct((128, 128), F32),
            jax.ShapeDtypeStruct((128, 128), F32),
        ),
        in_specs=[vmem] * 7,
        out_specs=(vmem,) * 2,
        scratch_shapes=[
            message, message, message, message, message, message,
            piece, piece, V((1, per, 128), F32), piece,
            V((16 * n, 128), BF16), V((128, 16 * n), BF16),
            V((256, 256), BF16), V((256, 256), BF16), V((256, 256), BF16),
            V((256, 256), BF16), V((256, 256), BF16),
            V((256, 128), F32), V((256, 128), F32),
            V((64, width + 256), BF16), V((64, width + 256), BF16), V((48, width + 256), F32),
            V((256, width), BF16), V((256, width), BF16), V((256, width), F32), V((256, width), F32),
            V((256, 256), F32), V((256, 256), F32), V((256, 256), F32), V((256, 128), F32),
            V((4, 256, 128), BF16), V((4, 256, 128), BF16),
            pltpu.SemaphoreType.DMA((5,)), pltpu.SemaphoreType.DMA((5,)),
        ],
        compiler_params=pltpu.CompilerParams(
            collective_id=0, has_side_effects=True, vmem_limit_bytes=63 << 20
        ),
        name="deblend",
    )(
        records.reshape(128, 128), dest.T, w_in.T, b_in.reshape(1, 64), w_mid, b_mid.reshape(1, 64), w_out.T
    )
    residual, dwi, dbi, dwm, dbm, dwo = pl.pallas_call(
        deal,
        out_shape=(
            jax.ShapeDtypeStruct((128, 128), F32),
            jax.ShapeDtypeStruct((36, 64), F32),
            jax.ShapeDtypeStruct((1, 64), F32),
            jax.ShapeDtypeStruct((64, 64), F32),
            jax.ShapeDtypeStruct((1, 64), F32),
            jax.ShapeDtypeStruct((36, 64), F32),
        ),
        in_specs=[vmem] * 2,
        out_specs=(vmem,) * 6,
        name="deal",
    )(*result)
    return (
        residual.reshape(records.shape),
        dwi.T,
        dbi.reshape(64),
        dwm,
        dbm.reshape(64),
        dwo.T,
    )


def solution(mesh):
    return jax.shard_map(
        functools.partial(local, mesh.shape["rec"]),
        mesh=mesh,
        in_specs=(
            P(None, ("groups", "rec"), None, None),
            P("groups", None),
            P(),
            P(),
            P(),
            P(),
            P(),
        ),
        out_specs=(
            P(None, ("groups", "rec"), None, None),
            P("groups", None),
            P("groups"),
            P("groups", None),
            P("groups"),
            P("groups", None),
        ),
        check_vma=False,
    )
```
